256 devices in a mesh: grp: 8 (over x, core), lx: 4 (over y), ly: 8 (over z).
Axes of the slice: x: 4, y: 4, z: 8, core: 2. Of those that a mesh axis runs over, the one named last changes fastest.
Arguments:
- vectors: float32 [32, 256, 4096], P('grp', 'lx', 'ly'), may hold values from -6 to 6
- levels: int32 [256, 4096], P('lx', 'ly'), may hold values from 0 to 7
- level_table: float32 [8], replicated, may hold values from 1 to 3
- filter_low: float32 [1], replicated, may hold values from -1 to 0.5
- filter_high: float32 [1], replicated, may hold values from 6 to 7.5
Outputs:
- basis: float32 [32, 256, 4096], P('grp', 'lx', 'ly')
The draws below stay inside these ranges and needn't reach their ends.
All inputs are finite; a program needn't handle non-finite values.
Results may differ from the reference program's by a relative error of at most 0.00011.
Values sent between devices are 32-bit elements; how exact they have to be, the bound alone decides.
No kernel may reach another device: no remote copies, remote signals or barrier semaphores. Data moves between devices by JAX's collectives and lax.ppermute only.
A program may use at most 64 MiB of HBM per device.

```python
import jax
import jax.numpy as jnp
from jax import lax

VB = 4
LEVELS = 8
NVEC = 32
NX = 256
NY = 4096
N_GRP = 8


def set_ends(array, key, least, high):
    index_at = [jax.random.randint(jax.random.fold_in(key, axis), (), 0, length) for axis, length in enumerate(array.shape)]
    main_axis = array.shape.index(max(array.shape))
    beside = index_at[:main_axis] + [(index_at[main_axis] + 1) % array.shape[main_axis]] + index_at[main_axis + 1:]
    return array.at[tuple(index_at)].set(least).at[tuple(beside)].set(high)


def block_levels(stream_key, dims, split, smallest, top_value):
    def one(axis_at, shards_of):
        heights = jax.random.uniform(jax.random.fold_in(jax.random.fold_in(stream_key, 6), axis_at), (shards_of,), jnp.float32, smallest / len(split), top_value / len(split))
        return jnp.repeat(jnp.exp(heights), dims[axis_at] // shards_of).reshape((-1,) + (1,) * (len(dims) - axis_at - 1))

    loudness = one(*split[0])
    for cut in split[1:]:
        loudness = loudness * one(*cut)
    return loudness


def scatter_about(own_key, shape, spread, reach, split=(), kind=jnp.bfloat16):
    drawn = spread * jax.random.normal(own_key, shape, jnp.float32)
    if split:
        drawn = drawn * block_levels(own_key, shape, split, -0.22, 0.18)
    return jnp.clip(drawn, -reach, reach).astype(kind)


def setup_inputs(seed: int = 0) -> dict:
    splits = jax.random.split(jax.random.key(seed), 6)
    return {
        "vectors": scatter_about(splits[0], (NVEC, NX, NY), 1.0, 6.0, ((0, 8), (1, 4), (2, 8)), jnp.float32),
        "levels": set_ends(jax.random.randint(splits[1], (NX, NY), 0, LEVELS), jax.random.fold_in(splits[1], 1), 0, LEVELS - 1).astype(jnp.int32),
        "level_table": jnp.clip(jax.random.uniform(splits[2], (LEVELS,), jnp.float32, 1.0, 3.0), 1.0, 3.0),
        "filter_low": jnp.clip(jax.random.uniform(splits[3], (1,), jnp.float32, -1.0, 0.5), -1.0, 0.5),
        "filter_high": jnp.clip(jax.random.uniform(splits[4], (1,), jnp.float32, 6.0, 7.5), 6.0, 7.5),
    }


def apply_operator(field, onsite):
    beside = jnp.roll(field, 1, 1) + jnp.roll(field, -1, 1) + jnp.roll(field, 1, 2) + jnp.roll(field, -1, 2)
    return onsite[None] * field - beside

def reference(vectors, levels, level_table, filter_low, filter_high):
    onsite = jnp.take(level_table, levels, axis=0)
    center = (filter_high[0] + filter_low[0]) / 2.0
    half = (filter_high[0] - filter_low[0]) / 2.0
    first = (apply_operator(vectors, onsite) - center * vectors) / half
    filtered = 2.0 * (apply_operator(first, onsite) - center * first) / half - vectors
    total = NX * NY
    blocks = [filtered[g * VB:(g + 1) * VB].reshape(VB, total) for g in range(N_GRP)]
    finished = []
    eye_small = jnp.eye(VB, dtype=jnp.float32)
    for h in range(N_GRP):
        current = blocks[h]
        gram = jnp.dot(current, current.T, precision=lax.Precision.HIGHEST) / total
        lower = jnp.linalg.cholesky(gram)
        inverse = lax.linalg.triangular_solve(lower, eye_small, left_side=True, lower=True)
        done = jnp.dot(inverse, current, precision=lax.Precision.HIGHEST)
        finished.append(done)
        for g in range(h + 1, N_GRP):
            coeff = jnp.dot(done, blocks[g].T, precision=lax.Precision.HIGHEST) / total
            blocks[g] = blocks[g] - jnp.dot(coeff.T, done, precision=lax.Precision.HIGHEST)
    return jnp.concatenate(finished, axis=0).reshape(NVEC, NX, NY)
```

```python
import jax
import jax.numpy as jnp
from jax import lax
from jax.experimental import pallas as pl
from jax.experimental.pallas import tpu as pltpu
from jax.sharding import PartitionSpec as P

HIGHEST = lax.Precision.HIGHEST
VMEM = pl.BlockSpec(memory_space=pltpu.VMEM)
SMEM = pl.BlockSpec(memory_space=pltpu.SMEM)


def shape_of(*dims):
    return jax.ShapeDtypeStruct(dims, jnp.float32)


def edge_rows_kernel(v_ref, levels_ref, table_ref, onsite_ref, first_ref, last_ref):
    levels = levels_ref[...]
    onsite = jnp.zeros(levels.shape, jnp.float32)
    for k in range(table_ref.shape[0]):
        onsite = jnp.where(levels == k, table_ref[k], onsite)
    onsite_ref[...] = onsite
    count, rows = v_ref.shape[0], v_ref.shape[1]
    for j in range(count):
        first_ref[2 * j : 2 * j + 2, :] = v_ref[j, 0:2, :]
        last_ref[2 * j : 2 * j + 2, :] = v_ref[j, rows - 2 : rows, :]
    first_ref[2 * count : 2 * count + 2, :] = onsite[0:2]
    last_ref[2 * count : 2 * count + 2, :] = onsite[rows - 2 : rows]


def halo_rows(above_ref, below_ref, j, lanes):
    width = lanes.stop - lanes.start
    gap = jnp.zeros((4, width), jnp.float32)
    return jnp.concatenate(
        [below_ref[2 * j : 2 * j + 2, lanes], gap, above_ref[2 * j : 2 * j + 2, lanes]], axis=0
    )


def edge_columns_kernel(v_ref, onsite_ref, above_ref, below_ref, first_ref, last_ref):
    count, rows, cols = v_ref.shape
    lane = lax.broadcasted_iota(jnp.int32, (rows + 8, 128), 1)
    first = jnp.zeros((rows + 8, 128), jnp.float32)
    last = jnp.zeros((rows + 8, 128), jnp.float32)
    for j in range(count + 1):
        head, tail = slice(0, 128), slice(cols - 128, cols)
        own_head = v_ref[j, :, head] if j < count else onsite_ref[:, head]
        own_tail = v_ref[j, :, tail] if j < count else onsite_ref[:, tail]
        left = jnp.concatenate([own_head, halo_rows(above_ref, below_ref, j, head)], axis=0)
        right = jnp.concatenate([own_tail, halo_rows(above_ref, below_ref, j, tail)], axis=0)
        if j:
            left = pltpu.roll(left, 2 * j, 1)
            right = pltpu.roll(right, 128 - 2 * j, 1)
        first = jnp.where(lane // 2 == j, left, first)
        last = jnp.where((127 - lane) // 2 == j, right, last)
    first_ref[...] = first
    last_ref[...] = last


def filter_kernel(v_ref, onsite_ref, above_ref, below_ref, before_ref, after_ref, low_ref, high_ref, out_ref):
    count, rows, cols = v_ref.shape
    strips = out_ref.shape[0]
    deep = rows // strips
    lane = lax.broadcasted_iota(jnp.int32, (rows + 8, 128), 1)
    wide = slice(0, cols)

    def extended(j):
        own = v_ref[j] if j < count else onsite_ref[...]
        tall = jnp.concatenate([own, halo_rows(above_ref, below_ref, j, wide)], axis=0)
        after, before = after_ref[...], before_ref[...]
        if j:
            after = pltpu.roll(after, 128 - 2 * j, 1)
            before = pltpu.roll(before, 2 * j, 1)
        side = jnp.where(lane < 64, after, before)
        return jnp.concatenate([tall, side], axis=1)

    center = (high_ref[0] + low_ref[0]) / 2.0
    half = jnp.full((1, 1), (high_ref[0] - low_ref[0]) * 0.5, jnp.float32)
    scale = 1.0 / half
    weight = (extended(count) - center) * scale

    def scaled_operator(x):
        height, width = x.shape
        beside = (pltpu.roll(x, 1, 0) + pltpu.roll(x, height - 1, 0)) + (
            pltpu.roll(x, 1, 1) + pltpu.roll(x, width - 1, 1)
        )
        return weight * x - scale * beside

    for j in range(count):
        x = extended(j)
        filtered = 2.0 * scaled_operator(scaled_operator(x)) - x
        for s in range(strips):
            out_ref[s, j] = filtered[s * deep : (s + 1) * deep, :cols]


def gram_kernel(scale, x_ref, out_ref):
    count, deep, cols = x_ref.shape
    gram = jnp.zeros((count, 128), jnp.float32)
    none = jnp.zeros((128 - count, cols), jnp.float32)
    for r in range(deep):
        x = x_ref[:, r, :]
        gram = gram + lax.dot_general(
            x, jnp.concatenate([x, none], axis=0), (((1,), (1,)), ((), ())),
            precision=HIGHEST, preferred_element_type=jnp.float32,
        )
    packed = gram[0:8]
    for q in range(1, count // 8):
        packed = packed + pltpu.roll(gram[8 * q : 8 * q + 8], q * count, 1)
    out_ref[...] = packed * scale


def combine_kernel(gram_ref, x_ref, out_ref):
    count, deep, cols = x_ref.shape
    packed = gram_ref[0]
    for k in range(1, gram_ref.shape[0]):
        packed = packed + gram_ref[k]
    pieces = [packed] + [pltpu.roll(packed, 128 - q * count, 1) for q in range(1, count // 8)]
    row = lax.broadcasted_iota(jnp.int32, (count, 128), 0)
    lane = lax.broadcasted_iota(jnp.int32, (count, 128), 1)
    work = jnp.where(lane < count, jnp.concatenate(pieces, axis=0), 0.0)
    work = jnp.where(lane == row + count, 1.0, work)
    for j in range(count):
        pivot = work[j : j + 1, :]
        factor = work[:, j : j + 1] * (1.0 / work[j : j + 1, j : j + 1])
        work = work - jnp.where(row > j, factor, 0.0) * pivot
    diagonal = jnp.sum(jnp.where(lane == row, work, 0.0), axis=1, keepdims=True)
    work = work * (1.0 / jnp.sqrt(diagonal))
    inverse = pltpu.roll(work, 128 - count, 1)[:, :count]
    for r in range(deep):
        out_ref[:, r, :] = jnp.dot(
            inverse, x_ref[:, r, :], precision=HIGHEST, preferred_element_type=jnp.float32
        )


def shifted(value, axis, step):
    size = lax.axis_size(axis)
    return lax.ppermute(value, axis, [(i, (i + step) % size) for i in range(size)])


def gathered(value, axes):
    size = lax.axis_size(axes)
    return lax.all_to_all(jnp.broadcast_to(value[None], (size,) + value.shape), axes, 0, 0)


def body(vectors, levels, level_table, filter_low, filter_high):
    count, rows, cols = vectors.shape
    groups = lax.axis_size("grp")
    every = count * groups
    deep = rows // groups
    packed_rows = 8 * ((2 * (count + 1) + 7) // 8)
    onsite, first_rows, last_rows = pl.pallas_call(
        edge_rows_kernel,
        out_shape=(shape_of(rows, cols), shape_of(packed_rows, cols), shape_of(packed_rows, cols)),
        in_specs=[VMEM, VMEM, SMEM],
        out_specs=(VMEM, VMEM, VMEM),
        name="edge_rows",
    )(vectors, levels, level_table)
    above = shifted(last_rows, "lx", 1)
    below = shifted(first_rows, "lx", -1)
    first_cols, last_cols = pl.pallas_call(
        edge_columns_kernel,
        out_shape=(shape_of(rows + 8, 128), shape_of(rows + 8, 128)),
        in_specs=[VMEM] * 4,
        out_specs=(VMEM, VMEM),
        name="edge_columns",
    )(vectors, onsite, above, below)
    before = shifted(last_cols, "ly", 1)
    after = shifted(first_cols, "ly", -1)
    strips = pl.pallas_call(
        filter_kernel,
        out_shape=shape_of(groups, count, deep, cols),
        in_specs=[VMEM] * 6 + [SMEM] * 2,
        out_specs=VMEM,
        name="filter",
    )(vectors, onsite, above, below, before, after, filter_low, filter_high)
    mine = lax.all_to_all(strips, "grp", 0, 0).reshape(every, deep, cols)
    total = rows * cols * lax.axis_size("lx") * lax.axis_size("ly")
    gram = pl.pallas_call(
        lambda *refs: gram_kernel(1.0 / total, *refs),
        out_shape=shape_of(8, 128),
        in_specs=[VMEM],
        out_specs=VMEM,
        name="gram",
    )(mine)
    gram = jnp.sum(gathered(gram, ("lx", "ly")), axis=0)
    grams = gathered(gram, "grp")
    done = pl.pallas_call(
        combine_kernel,
        out_shape=shape_of(every, deep, cols),
        in_specs=[VMEM] * 2,
        out_specs=VMEM,
        name="combine",
    )(grams, mine)
    back = lax.all_to_all(done.reshape(groups, count, deep, cols), "grp", 0, 0)
    return back.transpose(1, 0, 2, 3).reshape(count, rows, cols)


def solution(mesh):
    in_specs = (P("grp", "lx", "ly"), P("lx", "ly"), P(), P(), P())
    out_specs = P("grp", "lx", "ly")
    return jax.shard_map(body, mesh=mesh, in_specs=in_specs, out_specs=out_specs, check_vma=False)
```

```python
import jax
import jax.numpy as jnp
from jax import lax
from jax.experimental import pallas as pl
from jax.experimental.pallas import tpu as pltpu
from jax.sharding import PartitionSpec as P

HIGHEST = lax.Precision.HIGHEST
VMEM = pl.BlockSpec(memory_space=pltpu.VMEM)
SMEM = pl.BlockSpec(memory_space=pltpu.SMEM)
COMPILER = pltpu.CompilerParams(vmem_limit_bytes=16 * 1024 * 1024)


def shape_of(*dims):
    return jax.ShapeDtypeStruct(dims, jnp.float32)


def vmem_shape_of(*dims):
    return pltpu.VMEM(dims, jnp.float32)


def onsite_of(levels, table_ref):
    onsite = jnp.zeros(levels.shape, jnp.float32)
    for k in range(table_ref.shape[0]):
        onsite = jnp.where(levels == k, table_ref[k], onsite)
    return onsite


def edge_rows_kernel(place_ref, top_ref, end_ref, top_levels_ref, end_levels_ref, table_ref, near_ref, far_ref):
    even = place_ref[1] == 0
    count, rows = top_ref.shape[0], top_ref.shape[1]
    top_onsite = onsite_of(top_levels_ref[...], table_ref)
    end_onsite = onsite_of(end_levels_ref[...], table_ref)
    for j in range(count + 1):
        first = top_ref[j, 0:2, :] if j < count else top_onsite[0:2]
        last = end_ref[j, rows - 2 : rows, :] if j < count else end_onsite[rows - 2 : rows]
        near_ref[2 * j : 2 * j + 2, :] = jnp.where(even, last, first)
        far_ref[2 * j : 2 * j + 2, :] = jnp.where(even, first, last)


def halo_rows(near_ref, far_ref, even, j, lanes):
    near, far = near_ref[2 * j : 2 * j + 2, lanes], far_ref[2 * j : 2 * j + 2, lanes]
    gap = jnp.zeros((4, lanes.stop - lanes.start), jnp.float32)
    return jnp.concatenate([jnp.where(even, near, far), gap, jnp.where(even, far, near)], axis=0)


def edge_columns_kernel(
    place_ref, left_ref, right_ref, left_levels_ref, right_levels_ref, table_ref, near_rows_ref, far_rows_ref, near_ref, far_ref
):
    even_row, even_col = place_ref[1] == 0, place_ref[2] == 0
    count, rows, _ = left_ref.shape
    cols = near_rows_ref.shape[1]
    lane = lax.broadcasted_iota(jnp.int32, (rows + 8, 128), 1)
    first = jnp.zeros((rows + 8, 128), jnp.float32)
    last = jnp.zeros((rows + 8, 128), jnp.float32)
    for j in range(count + 1):
        head, tail = slice(0, 128), slice(cols - 128, cols)
        own_head = left_ref[j] if j < count else onsite_of(left_levels_ref[...], table_ref)
        own_tail = right_ref[j] if j < count else onsite_of(right_levels_ref[...], table_ref)
        left = jnp.concatenate([own_head, halo_rows(near_rows_ref, far_rows_ref, even_row, j, head)], axis=0)
        right = jnp.concatenate([own_tail, halo_rows(near_rows_ref, far_rows_ref, even_row, j, tail)], axis=0)
        if j:
            left = pltpu.roll(left, 2 * j, 1)
            right = pltpu.roll(right, 128 - 2 * j, 1)
        first = jnp.where(lane // 2 == j, left, first)
        last = jnp.where((127 - lane) // 2 == j, right, last)
    near_ref[...] = jnp.where(even_col, last, first)
    far_ref[...] = jnp.where(even_col, first, last)


def filter_kernel(
    place_ref, v_ref, levels_ref, table_ref, near_rows_ref, far_rows_ref, near_ref, far_ref, low_ref, high_ref, out_ref
):
    even_row, even_col = place_ref[1] == 0, place_ref[2] == 0
    count, rows, cols = v_ref.shape
    strips = out_ref.shape[0]
    deep = rows // strips
    lane = lax.broadcasted_iota(jnp.int32, (rows + 8, 128), 1)
    wide = slice(0, cols)
    near, far = near_ref[...], far_ref[...]
    after = jnp.where(even_col, near, far)
    before = jnp.where(even_col, far, near)

    def extended(own, j):
        tall = jnp.concatenate([own, halo_rows(near_rows_ref, far_rows_ref, even_row, j, wide)], axis=0)
        right = pltpu.roll(after, 128 - 2 * j, 1) if j else after
        left = pltpu.roll(before, 2 * j, 1) if j else before
        return jnp.concatenate([tall, jnp.where(lane < 64, right, left)], axis=1)

    center = (high_ref[0] + low_ref[0]) / 2.0
    half = jnp.full((1, 1), (high_ref[0] - low_ref[0]) * 0.5, jnp.float32)
    scale = 1.0 / half
    weight = (extended(onsite_of(levels_ref[...], table_ref), count) - center) * scale

    def scaled_operator(x):
        height, width = x.shape
        beside = (pltpu.roll(x, 1, 0) + pltpu.roll(x, height - 1, 0)) + (
            pltpu.roll(x, 1, 1) + pltpu.roll(x, width - 1, 1)
        )
        return weight * x - scale * beside

    for j in range(count):
        x = extended(v_ref[j], j)
        filtered = 2.0 * scaled_operator(scaled_operator(x)) - x
        for s in range(strips):
            out_ref[s, j] = filtered[s * deep : (s + 1) * deep, :cols]


def gram_kernel(scale, x_ref, out_ref):
    count, deep, cols = x_ref.shape
    gram = jnp.zeros((count, 128), jnp.float32)
    none = jnp.zeros((128 - count, cols), jnp.float32)
    for r in range(deep):
        x = x_ref[:, r, :]
        gram = gram + lax.dot_general(
            x, jnp.concatenate([x, none], axis=0), (((1,), (1,)), ((), ())),
            precision=HIGHEST, preferred_element_type=jnp.float32,
        )
    packed = gram[0:8]
    for q in range(1, count // 8):
        packed = packed + pltpu.roll(gram[8 * q : 8 * q + 8], q * count, 1)
    out_ref[...] = jnp.broadcast_to((packed * scale)[None], out_ref.shape)


def factor_kernel(gram_ref, place_ref, factors_ref):
    count, every, _ = factors_ref.shape
    packed = gram_ref[0]
    for k in range(1, gram_ref.shape[0]):
        packed = packed + gram_ref[k]
    pieces = [packed] + [pltpu.roll(packed, 128 - q * every, 1) for q in range(1, every // 8)]
    row = lax.broadcasted_iota(jnp.int32, (every, 128), 0)
    lane = lax.broadcasted_iota(jnp.int32, (every, 128), 1)
    work = jnp.where(lane < every, jnp.concatenate(pieces, axis=0), 0.0)
    work = jnp.where(lane == row + every, 1.0, work)
    for j in range(every):
        pivot = work[j : j + 1, :]
        factor = work[:, j : j + 1] * (1.0 / work[j : j + 1, j : j + 1])
        work = work - jnp.where(row > j, factor, 0.0) * pivot
    diagonal = jnp.sum(jnp.where(lane == row, work, 0.0), axis=1, keepdims=True)
    inverse = work * (1.0 / jnp.sqrt(diagonal))
    for i in range(count):
        mine = jnp.sum(jnp.where(row == place_ref[0] * count + i, inverse, 0.0), axis=0, keepdims=True)
        upright = jnp.sum(jnp.where(lane == row + every, mine, 0.0), axis=1, keepdims=True)
        factors_ref[i] = jnp.broadcast_to(upright, (every, 128))


def combine_kernel(factors_ref, place_ref, *refs):
    *tiles, out_ref = refs
    strips, count, deep, cols = tiles[0].shape
    own = place_ref[0]

    def one_strip(s, carry):
        for c in range(cols // 128):
            lanes = slice(c * 128, c * 128 + 128)
            totals = [jnp.zeros((deep, 128), jnp.float32) for _ in range(count)]
            for q, tile in enumerate(tiles):
                first = (own ^ q) * count
                for k in range(count):
                    x = tile[s, k, :, lanes]
                    for i in range(count):
                        totals[i] = totals[i] + factors_ref[i, pl.ds(first + k, deep, stride=0), :] * x
            for i in range(count):
                out_ref[i, pl.ds(pl.multiple_of(s * deep, deep), deep), lanes] = totals[i]
        return carry

    lax.fori_loop(0, strips, one_strip, 0)


def swapped(value, axis, partner):
    return lax.ppermute(value, axis, [(i, partner(i)) for i in range(lax.axis_size(axis))])


def near_and_far(near, far, axis):
    size = lax.axis_size(axis)
    other = swapped(far, axis, lambda i: (i + (1 if i % 2 else -1)) % size)
    return swapped(near, axis, lambda i: i ^ 1), other


def in_vmem(*values):
    return [pltpu.with_memory_space_constraint(v, pltpu.VMEM) for v in values]


def body(vectors, levels, level_table, filter_low, filter_high):
    count, rows, cols = vectors.shape
    groups = lax.axis_size("grp")
    every = count * groups
    deep = rows // groups
    packed_rows = 8 * ((2 * (count + 1) + 7) // 8)
    place = jnp.stack([lax.axis_index("grp"), lax.axis_index("lx") % 2, lax.axis_index("ly") % 2])
    row_ends, col_ends = rows // 8 - 1, cols // 128 - 1
    hbm_vectors, hbm_levels = (pltpu.with_memory_space_constraint(v, pltpu.HBM) for v in (vectors, levels))
    near_rows, far_rows = pl.pallas_call(
        edge_rows_kernel,
        grid=(1,),
        out_shape=(vmem_shape_of(packed_rows, cols), vmem_shape_of(packed_rows, cols)),
        in_specs=[
            SMEM,
            pl.BlockSpec((count, 8, cols), lambda i: (0, 0, 0)),
            pl.BlockSpec((count, 8, cols), lambda i: (0, row_ends, 0)),
            pl.BlockSpec((8, cols), lambda i: (0, 0)),
            pl.BlockSpec((8, cols), lambda i: (row_ends, 0)),
            SMEM,
        ],
        out_specs=(VMEM, VMEM),
        compiler_params=COMPILER,
        name="edge_rows",
    )(place, hbm_vectors, hbm_vectors, hbm_levels, hbm_levels, level_table)
    near_rows, far_rows = in_vmem(*near_and_far(near_rows, far_rows, "lx"))
    near, far = pl.pallas_call(
        edge_columns_kernel,
        grid=(1,),
        out_shape=(vmem_shape_of(rows + 8, 128), vmem_shape_of(rows + 8, 128)),
        in_specs=[
            SMEM,
            pl.BlockSpec((count, rows, 128), lambda i: (0, 0, 0)),
            pl.BlockSpec((count, rows, 128), lambda i: (0, 0, col_ends)),
            pl.BlockSpec((rows, 128), lambda i: (0, 0)),
            pl.BlockSpec((rows, 128), lambda i: (0, col_ends)),
            SMEM,
            VMEM,
            VMEM,
        ],
        out_specs=(VMEM, VMEM),
        compiler_params=COMPILER,
        name="edge_columns",
    )(place, vectors, vectors, levels, levels, level_table, near_rows, far_rows)
    near, far = in_vmem(*near_and_far(near, far, "ly"))
    strips = pl.pallas_call(
        filter_kernel,
        out_shape=vmem_shape_of(groups, count, deep, cols),
        in_specs=[SMEM, VMEM, VMEM, SMEM] + [VMEM] * 4 + [SMEM] * 2,
        out_specs=VMEM,
        compiler_params=COMPILER,
        name="filter",
    )(place, vectors, levels, level_table, near_rows, far_rows, near, far, filter_low, filter_high)
    mine = lax.all_to_all(strips, "grp", 0, 0).reshape(every, deep, cols)
    strips, mine = lax.optimization_barrier((strips, mine))
    tiles = {0: strips, 1: swapped(strips, "grp", lambda i: i ^ 1)}
    for q in range(2, groups, 2):
        tiles[q] = swapped(strips, "grp", lambda i: i ^ q)
    planes = lax.axis_size("lx") * lax.axis_size("ly")
    total = rows * cols * planes
    gram = pl.pallas_call(
        lambda *refs: gram_kernel(1.0 / total, *refs),
        out_shape=vmem_shape_of(planes, 8, 128),
        in_specs=[VMEM],
        out_specs=VMEM,
        compiler_params=COMPILER,
        name="gram",
    )(*in_vmem(mine))
    gram = jnp.sum(lax.all_to_all(gram, ("lx", "ly"), 0, 0), axis=0)
    grams = lax.all_to_all(jnp.broadcast_to(gram[None], (groups,) + gram.shape), "grp", 0, 0)
    grams, tiles = lax.optimization_barrier((grams, tiles))
    for q in range(2, groups, 2):
        tiles[q + 1] = swapped(tiles[q], "grp", lambda i: i ^ 1)
    factors = pl.pallas_call(
        factor_kernel,
        out_shape=vmem_shape_of(count, every, 128),
        in_specs=[VMEM, SMEM],
        out_specs=VMEM,
        compiler_params=COMPILER,
        name="factor",
    )(*in_vmem(grams), place)
    return pl.pallas_call(
        combine_kernel,
        out_shape=shape_of(count, rows, cols),
        in_specs=[VMEM, SMEM] + [VMEM] * groups,
        out_specs=VMEM,
        compiler_params=COMPILER,
        name="combine",
    )(factors, place, *in_vmem(*[tiles[q] for q in range(groups)]))


def solution(mesh):
    in_specs = (P("grp", "lx", "ly"), P("lx", "ly"), P(), P(), P())
    out_specs = P("grp", "lx", "ly")
    return jax.shard_map(body, mesh=mesh, in_specs=in_specs, out_specs=out_specs, check_vma=False)
```

```python
import jax
import jax.numpy as jnp
from jax import lax
from jax.experimental import pallas as pl
from jax.experimental.pallas import tpu as pltpu
from jax.sharding import PartitionSpec as P

HIGHEST = lax.Precision.HIGHEST
VMEM = pl.BlockSpec(memory_space=pltpu.VMEM)
SMEM = pl.BlockSpec(memory_space=pltpu.SMEM)
COMPILER = pltpu.CompilerParams(vmem_limit_bytes=16 * 1024 * 1024)


def shape_of(*dims):
    return jax.ShapeDtypeStruct(dims, jnp.float32)


def vmem_shape_of(*dims):
    return pltpu.VMEM(dims, jnp.float32)


def onsite_of(levels, table_ref):
    onsite = jnp.zeros(levels.shape, jnp.float32)
    for k in range(table_ref.shape[0]):
        onsite = jnp.where(levels == k, table_ref[k], onsite)
    return onsite


def edge_rows_kernel(place_ref, top_ref, end_ref, top_levels_ref, end_levels_ref, near_ref, far_ref):
    even = place_ref[1] == 0
    count, rows = top_ref.shape[0], top_ref.shape[1]
    top_levels = top_levels_ref[...].astype(jnp.float32)
    end_levels = end_levels_ref[...].astype(jnp.float32)
    for j in range(count + 1):
        first = top_ref[j, 0:2, :] if j < count else top_levels[0:2]
        last = end_ref[j, rows - 2 : rows, :] if j < count else end_levels[rows - 2 : rows]
        near_ref[2 * j : 2 * j + 2, :] = jnp.where(even, last, first)
        far_ref[2 * j : 2 * j + 2, :] = jnp.where(even, first, last)


def halo_rows(near_ref, far_ref, even, j, lanes):
    near, far = near_ref[2 * j : 2 * j + 2, lanes], far_ref[2 * j : 2 * j + 2, lanes]
    gap = jnp.zeros((4, lanes.stop - lanes.start), jnp.float32)
    return jnp.concatenate([jnp.where(even, near, far), gap, jnp.where(even, far, near)], axis=0)


def edge_columns_kernel(
    place_ref, left_ref, right_ref, left_levels_ref, right_levels_ref, near_rows_ref, far_rows_ref, near_ref, far_ref
):
    even_row, even_col = place_ref[1] == 0, place_ref[2] == 0
    count, rows, _ = left_ref.shape
    cols = near_rows_ref.shape[1]
    lane = lax.broadcasted_iota(jnp.int32, (rows + 8, 128), 1)
    first = jnp.zeros((rows + 8, 128), jnp.float32)
    last = jnp.zeros((rows + 8, 128), jnp.float32)
    for j in range(count + 1):
        head, tail = slice(0, 128), slice(cols - 128, cols)
        own_head = left_ref[j] if j < count else left_levels_ref[...].astype(jnp.float32)
        own_tail = right_ref[j] if j < count else right_levels_ref[...].astype(jnp.float32)
        left = jnp.concatenate([own_head, halo_rows(near_rows_ref, far_rows_ref, even_row, j, head)], axis=0)
        right = jnp.concatenate([own_tail, halo_rows(near_rows_ref, far_rows_ref, even_row, j, tail)], axis=0)
        if j:
            left = pltpu.roll(left, 2 * j, 1)
            right = pltpu.roll(right, 128 - 2 * j, 1)
        first = jnp.where(lane // 2 == j, left, first)
        last = jnp.where((127 - lane) // 2 == j, right, last)
    near_ref[...] = jnp.where(even_col, last, first)
    far_ref[...] = jnp.where(even_col, first, last)


def filter_kernel(
    place_ref, v_ref, levels_ref, table_ref, near_rows_ref, far_rows_ref, near_ref, far_ref, low_ref, high_ref, out_ref
):
    even_row, even_col = place_ref[1] == 0, place_ref[2] == 0
    count, rows, cols = v_ref.shape
    strips = out_ref.shape[0]
    deep = rows // strips
    lane = lax.broadcasted_iota(jnp.int32, (rows + 8, 128), 1)
    wide = slice(0, cols)
    near, far = near_ref[...], far_ref[...]
    after = jnp.where(even_col, near, far)
    before = jnp.where(even_col, far, near)

    def extended(own, j):
        tall = jnp.concatenate([own, halo_rows(near_rows_ref, far_rows_ref, even_row, j, wide)], axis=0)
        right = pltpu.roll(after, 128 - 2 * j, 1) if j else after
        left = pltpu.roll(before, 2 * j, 1) if j else before
        return jnp.concatenate([tall, jnp.where(lane < 64, right, left)], axis=1)

    center = (high_ref[0] + low_ref[0]) / 2.0
    half = jnp.full((1, 1), (high_ref[0] - low_ref[0]) * 0.5, jnp.float32)
    scale = 1.0 / half
    weight = (onsite_of(extended(levels_ref[...].astype(jnp.float32), count), table_ref) - center) * scale

    def scaled_operator(x):
        height, width = x.shape
        beside = (pltpu.roll(x, 1, 0) + pltpu.roll(x, height - 1, 0)) + (
            pltpu.roll(x, 1, 1) + pltpu.roll(x, width - 1, 1)
        )
        return weight * x - scale * beside

    for j in range(count):
        x = extended(v_ref[j], j)
        filtered = 2.0 * scaled_operator(scaled_operator(x)) - x
        for s in range(strips):
            out_ref[s, j] = filtered[s * deep : (s + 1) * deep, :cols]


def gram_kernel(scale, x_ref, out_ref):
    count, deep, cols = x_ref.shape
    gram = jnp.zeros((count, 128), jnp.float32)
    none = jnp.zeros((128 - count, cols), jnp.float32)
    for r in range(deep):
        x = x_ref[:, r, :]
        gram = gram + lax.dot_general(
            x, jnp.concatenate([x, none], axis=0), (((1,), (1,)), ((), ())),
            precision=HIGHEST, preferred_element_type=jnp.float32,
        )
    packed = gram[0:8]
    for q in range(1, count // 8):
        packed = packed + pltpu.roll(gram[8 * q : 8 * q + 8], q * count, 1)
    out_ref[...] = jnp.broadcast_to((packed * scale)[None], out_ref.shape)


def spread_lane(x, j):
    return jnp.broadcast_to(x[:, j : j + 1], x.shape)


def factor_kernel(gram_ref, place_ref, factors_ref):
    count, every, _ = factors_ref.shape
    packed = gram_ref[0]
    for k in range(1, gram_ref.shape[0]):
        packed = packed + gram_ref[k]
    pieces = [packed] + [pltpu.roll(packed, 128 - q * every, 1) for q in range(1, every // 8)]
    row = lax.broadcasted_iota(jnp.int32, (every, 128), 0)
    lane = lax.broadcasted_iota(jnp.int32, (every, 128), 1)
    work = jnp.where(lane < every, jnp.concatenate(pieces, axis=0), 0.0)
    work = jnp.where(lane == row + every, 1.0, work)
    for j in range(0, every, 2):
        top, next_row = work[j : j + 1, :], work[j + 1 : j + 2, :]
        p, q, r = spread_lane(top, j), spread_lane(top, j + 1), spread_lane(next_row, j + 1)
        inverse_p, inverse_det = 1.0 / p, 1.0 / (p * r - q * q)
        first, second = (top * r - next_row * q) * inverse_det, (next_row * p - top * q) * inverse_det
        left, right = spread_lane(work, j), spread_lane(work, j + 1)
        below = row > j + 1
        update = jnp.where(below, left, 0.0) * first + jnp.where(below, right, 0.0) * second
        work = work - update - jnp.where(row == j + 1, left, 0.0) * (top * inverse_p)
    diagonal = jnp.sum(jnp.where(lane == row, work, 0.0), axis=1, keepdims=True)
    inverse = work * (1.0 / jnp.sqrt(diagonal))
    for i in range(count):
        mine = jnp.sum(jnp.where(row == place_ref[0] * count + i, inverse, 0.0), axis=0, keepdims=True)
        upright = jnp.sum(jnp.where(lane == row + every, mine, 0.0), axis=1, keepdims=True)
        factors_ref[i] = jnp.broadcast_to(upright, (every, 128))


def combine_kernel(factors_ref, place_ref, *refs):
    *tiles, out_ref = refs
    strips, count, deep, cols = tiles[0].shape
    starts = [(place_ref[0] ^ q) * count for q in range(len(tiles))]

    def one_strip(s, carry):
        rows = pl.ds(pl.multiple_of(s * deep, deep), deep)
        for c in range(0, cols, 256):
            parts = [slice(c, c + 128), slice(c + 128, c + 256)]
            totals = [[jnp.zeros((deep, 128), jnp.float32) for _ in parts] for _ in range(count)]
            for start, tile in zip(starts, tiles):
                for k in range(count):
                    fields = [tile[s, k, :, lanes] for lanes in parts]
                    for i in range(count):
                        factor = factors_ref[i, pl.ds(start + k, deep, stride=0), :]
                        totals[i] = [total + factor * field for total, field in zip(totals[i], fields)]
            for i in range(count):
                for lanes, total in zip(parts, totals[i]):
                    out_ref[i, rows, lanes] = total
        return carry

    lax.fori_loop(0, strips, one_strip, 0, unroll=True)


def swapped(value, axis, partner):
    return lax.ppermute(value, axis, [(i, partner(i)) for i in range(lax.axis_size(axis))])


def near_and_far(near, far, axis):
    size = lax.axis_size(axis)
    near = swapped(near, axis, lambda i: i ^ 1)
    return near, swapped(far, axis, lambda i: (i + (1 if i % 2 else -1)) % size)


def in_vmem(*values):
    return [pltpu.with_memory_space_constraint(v, pltpu.VMEM) for v in values]


def body(vectors, levels, level_table, filter_low, filter_high):
    count, rows, cols = vectors.shape
    groups = lax.axis_size("grp")
    every = count * groups
    deep = rows // groups
    packed_rows = 8 * ((2 * (count + 1) + 7) // 8)
    place = jnp.stack([lax.axis_index("grp"), lax.axis_index("lx") % 2, lax.axis_index("ly") % 2])
    row_ends, col_ends = rows // 8 - 1, cols // 128 - 1
    hbm_vectors, hbm_levels = (pltpu.with_memory_space_constraint(v, pltpu.HBM) for v in (vectors, levels))
    near_rows, far_rows = pl.pallas_call(
        edge_rows_kernel,
        grid=(1,),
        out_shape=(vmem_shape_of(packed_rows, cols), vmem_shape_of(packed_rows, cols)),
        in_specs=[
            SMEM,
            pl.BlockSpec((count, 8, cols), lambda i: (0, 0, 0)),
            pl.BlockSpec((count, 8, cols), lambda i: (0, row_ends, 0)),
            pl.BlockSpec((8, cols), lambda i: (0, 0)),
            pl.BlockSpec((8, cols), lambda i: (row_ends, 0)),
        ],
        out_specs=(VMEM, VMEM),
        compiler_params=COMPILER,
        name="edge_rows",
    )(place, hbm_vectors, hbm_vectors, hbm_levels, hbm_levels)
    near_rows, far_rows = in_vmem(*near_and_far(near_rows, far_rows, "lx"))
    near, far = pl.pallas_call(
        edge_columns_kernel,
        grid=(1,),
        out_shape=(vmem_shape_of(rows + 8, 128), vmem_shape_of(rows + 8, 128)),
        in_specs=[
            SMEM,
            pl.BlockSpec((count, rows, 128), lambda i: (0, 0, 0)),
            pl.BlockSpec((count, rows, 128), lambda i: (0, 0, col_ends)),
            pl.BlockSpec((rows, 128), lambda i: (0, 0)),
            pl.BlockSpec((rows, 128), lambda i: (0, col_ends)),
            VMEM,
            VMEM,
        ],
        out_specs=(VMEM, VMEM),
        compiler_params=COMPILER,
        name="edge_columns",
    )(place, vectors, vectors, levels, levels, near_rows, far_rows)
    near, far = in_vmem(*near_and_far(near, far, "ly"))
    strips = pl.pallas_call(
        filter_kernel,
        out_shape=vmem_shape_of(groups, count, deep, cols),
        in_specs=[SMEM, VMEM, VMEM, SMEM] + [VMEM] * 4 + [SMEM] * 2,
        out_specs=VMEM,
        compiler_params=COMPILER,
        name="filter",
    )(place, vectors, levels, level_table, near_rows, far_rows, near, far, filter_low, filter_high)
    mine = lax.all_to_all(strips, "grp", 0, 0).reshape(every, deep, cols)
    strips, mine = lax.optimization_barrier((strips, mine))
    tiles = {q: swapped(strips, "grp", lambda i, q=q: i ^ q) for q in (1, 4, 2, 6)}
    tiles[0] = strips
    planes = lax.axis_size("lx") * lax.axis_size("ly")
    total = rows * cols * planes
    gram = pl.pallas_call(
        lambda *refs: gram_kernel(1.0 / total, *refs),
        out_shape=vmem_shape_of(planes, 8, 128),
        in_specs=[VMEM],
        out_specs=VMEM,
        compiler_params=COMPILER,
        name="gram",
    )(*in_vmem(mine))
    gram = jnp.sum(lax.all_to_all(gram, ("lx", "ly"), 0, 0), axis=0)
    grams = lax.all_to_all(jnp.broadcast_to(gram[None], (groups,) + gram.shape), "grp", 0, 0)
    grams, tiles = lax.optimization_barrier((grams, tiles))
    for q in range(2, groups, 2):
        tiles[q + 1] = swapped(tiles[q], "grp", lambda i: i ^ 1)
    factors = pl.pallas_call(
        factor_kernel,
        out_shape=vmem_shape_of(count, every, 128),
        in_specs=[VMEM, SMEM],
        out_specs=VMEM,
        compiler_params=COMPILER,
        name="factor",
    )(*in_vmem(grams), place)
    return pl.pallas_call(
        combine_kernel,
        out_shape=shape_of(count, rows, cols),
        in_specs=[VMEM, SMEM] + [VMEM] * groups,
        out_specs=VMEM,
        compiler_params=COMPILER,
        name="combine",
    )(factors, place, *in_vmem(*[tiles[q] for q in range(groups)]))


def solution(mesh):
    in_specs = (P("grp", "lx", "ly"), P("lx", "ly"), P(), P(), P())
    out_specs = P("grp", "lx", "ly")
    return jax.shard_map(body, mesh=mesh, in_specs=in_specs, out_specs=out_specs, check_vma=False)
```

```python
import jax
import jax.numpy as jnp
from jax import lax
from jax.experimental import pallas as pl
from jax.experimental.pallas import tpu as pltpu
from jax.sharding import PartitionSpec as P

HIGHEST = lax.Precision.HIGHEST
VMEM = pl.BlockSpec(memory_space=pltpu.VMEM)
SMEM = pl.BlockSpec(memory_space=pltpu.SMEM)
COMPILER = pltpu.CompilerParams(vmem_limit_bytes=16 * 1024 * 1024)


def shape_of(*dims):
    return jax.ShapeDtypeStruct(dims, jnp.float32)


def vmem_shape_of(*dims):
    return pltpu.VMEM(dims, jnp.float32)


def onsite_of(levels, table_ref):
    onsite = jnp.zeros(levels.shape, jnp.float32)
    for k in range(table_ref.shape[0]):
        onsite = jnp.where(levels == k, table_ref[k], onsite)
    return onsite


def halo_rows(near_ref, far_ref, even, j, parts, chosen):
    tiles = []
    for c in chosen:
        at = 2 * (j * parts + c)
        near, far = near_ref[at : at + 2, :], far_ref[at : at + 2, :]
        tiles.append(
            jnp.concatenate(
                [jnp.where(even, near, far), jnp.zeros((4, 128), jnp.float32), jnp.where(even, far, near)], axis=0
            )
        )
    return jnp.concatenate(tiles, axis=1)


def packed_lanes(x):
    groups = x.shape[0] // 8
    blocks = []
    for start in range(0, groups, 8):
        block = x[8 * start : 8 * start + 8]
        for t in range(1, min(8, groups - start)):
            block = block + pltpu.roll(x[8 * (start + t) : 8 * (start + t) + 8], 16 * t, 1)
        blocks.append(block)
    return jnp.concatenate(blocks, axis=1)


def unpacked_lanes(x, groups):
    tiles = []
    for t in range(groups):
        block = x[:, 128 * (t // 8) : 128 * (t // 8) + 128]
        tiles.append(pltpu.roll(block, 128 - 16 * (t % 8), 1) if t % 8 else block)
    return jnp.concatenate(tiles, axis=0)


def edges_kernel(
    place_ref, top_ref, end_ref, left_ref, right_ref, top_levels_ref, end_levels_ref, left_levels_ref, right_levels_ref,
    near_rows_ref, far_rows_ref, near_cols_ref, far_cols_ref,
):
    even_row, even_col = place_ref[1] == 0, place_ref[2] == 0
    count, deep = top_ref.shape[0], top_ref.shape[1]
    parts = top_ref.shape[2] // 128
    top_levels = top_levels_ref[...].astype(jnp.float32)
    end_levels = end_levels_ref[...].astype(jnp.float32)
    for j in range(count + 1):
        first = top_ref[j, 0:2, :] if j < count else top_levels[0:2]
        last = end_ref[j, deep - 2 : deep, :] if j < count else end_levels[deep - 2 : deep]
        near, far = jnp.where(even_row, last, first), jnp.where(even_row, first, last)
        for c in range(parts):
            at = 2 * (j * parts + c)
            near_rows_ref[at : at + 2, :] = near[:, c * 128 : c * 128 + 128]
            far_rows_ref[at : at + 2, :] = far[:, c * 128 : c * 128 + 128]
    rows = left_ref.shape[1]
    lane = lax.broadcasted_iota(jnp.int32, (rows, 128), 1)
    first = jnp.zeros((rows, 128), jnp.float32)
    last = jnp.zeros((rows, 128), jnp.float32)
    for j in range(count + 1):
        left = left_ref[j] if j < count else left_levels_ref[...].astype(jnp.float32)
        right = right_ref[j] if j < count else right_levels_ref[...].astype(jnp.float32)
        if j:
            left = pltpu.roll(left, 2 * j, 1)
            right = pltpu.roll(right, 128 - 2 * j, 1)
        first = jnp.where(lane // 2 == j, left, first)
        last = jnp.where((127 - lane) // 2 == j, right, last)
    first, last = packed_lanes(first), packed_lanes(last)
    near_cols_ref[...] = jnp.where(even_col, last, first)
    far_cols_ref[...] = jnp.where(even_col, first, last)


def filter_kernel(
    place_ref, v_ref, levels_ref, table_ref, near_rows_ref, far_rows_ref, near_ref, far_ref, low_ref, high_ref, out_ref, corner_ref
):
    even_row, even_col = place_ref[1] == 0, place_ref[2] == 0
    count, rows, cols = v_ref.shape
    strips = out_ref.shape[0]
    deep = rows // strips
    lane = lax.broadcasted_iota(jnp.int32, (rows, 128), 1)
    parts = cols // 128
    near, far = near_ref[...], far_ref[...]
    after = unpacked_lanes(jnp.where(even_col, near, far), rows // 8)
    before = unpacked_lanes(jnp.where(even_col, far, near), rows // 8)

    def extended(own, j):
        tall = jnp.concatenate([own, halo_rows(near_rows_ref, far_rows_ref, even_row, j, parts, range(parts))], axis=0)
        right = pltpu.roll(after, 128 - 2 * j, 1) if j else after
        left = pltpu.roll(before, 2 * j, 1) if j else before
        side = jnp.concatenate([jnp.where(lane < 64, right, left), jnp.zeros((8, 128), jnp.float32)], axis=0)
        return jnp.concatenate([tall, side], axis=1)

    center = (high_ref[0] + low_ref[0]) / 2.0
    half = jnp.full((1, 1), (high_ref[0] - low_ref[0]) * 0.5, jnp.float32)
    scale = 1.0 / half
    weight = (onsite_of(extended(levels_ref[...].astype(jnp.float32), count), table_ref) - center) * scale

    def scaled_operator(x):
        height, width = x.shape
        beside = (pltpu.roll(x, 1, 0) + pltpu.roll(x, height - 1, 0)) + (
            pltpu.roll(x, 1, 1) + pltpu.roll(x, width - 1, 1)
        )
        return weight * x - scale * beside

    site = lax.broadcasted_iota(jnp.int32, (1, 128), 1)
    row_at = lax.broadcasted_iota(jnp.int32, (rows, cols), 0)
    col_at = lax.broadcasted_iota(jnp.int32, (rows, cols), 1)
    inside = ((row_at > 0) & (row_at < rows - 1)) | ((col_at > 0) & (col_at < cols - 1))
    corners = [(0, 0), (0, cols - 1), (rows - 1, 0), (rows - 1, cols - 1)]
    corner_ref[...] = jnp.zeros(corner_ref.shape, jnp.float32)
    for j in range(count):
        own = v_ref[j]
        x = extended(own, j)
        filtered = (2.0 * scaled_operator(scaled_operator(x)) - x)[:rows, :cols]
        held = jnp.zeros((1, 128), jnp.float32)
        for c, (r, l) in enumerate(corners):
            held = held + jnp.where(site == place_ref[3] + c, filtered[r : r + 1, l : l + 1], 0.0)
            held = held + jnp.where(site == place_ref[4 + c], 4.0 * scale * scale * own[r : r + 1, l : l + 1], 0.0)
        corner_ref[j : j + 1, :] = held
        filtered = jnp.where(inside, filtered, 0.0)
        for s in range(strips):
            out_ref[s, j] = filtered[s * deep : (s + 1) * deep]


def gram_kernel(scale, x_ref, corner_ref, out_ref):
    count, deep, cols = x_ref.shape
    gram = jnp.zeros((count, 128), jnp.float32)
    none = jnp.zeros((128 - count, cols), jnp.float32)
    for r in range(deep):
        x = x_ref[:, r, :]
        gram = gram + lax.dot_general(
            x, jnp.concatenate([x, none], axis=0), (((1,), (1,)), ((), ())),
            precision=HIGHEST, preferred_element_type=jnp.float32,
        )
    packed = gram[0:8]
    for q in range(1, count // 8):
        packed = packed + pltpu.roll(gram[8 * q : 8 * q + 8], q * count, 1)
    both = jnp.concatenate([packed * scale, corner_ref[0 : out_ref.shape[1] - 8, :]], axis=0)
    out_ref[...] = jnp.broadcast_to(both[None], out_ref.shape)


def spread_lane(x, j):
    return jnp.broadcast_to(x[:, j : j + 1], x.shape)


def factor_kernel(scale, gram_ref, place_ref, factors_ref, corners_ref):
    count, every, _ = factors_ref.shape
    packed = gram_ref[0, 0:8, :]
    for k in range(1, gram_ref.shape[0]):
        packed = packed + gram_ref[k, 0:8, :]
    sites = jnp.concatenate([gram_ref[k, 8 : 8 + count, :] for k in range(gram_ref.shape[0])], axis=0)
    none = jnp.zeros((128 - every, 128), jnp.float32)
    at_corners = lax.dot_general(
        sites, jnp.concatenate([sites, none], axis=0), (((1,), (1,)), ((), ())),
        precision=HIGHEST, preferred_element_type=jnp.float32,
    )
    pieces = [packed] + [pltpu.roll(packed, 128 - q * every, 1) for q in range(1, every // 8)]
    row = lax.broadcasted_iota(jnp.int32, (every, 128), 0)
    lane = lax.broadcasted_iota(jnp.int32, (every, 128), 1)
    work = jnp.where(lane < every, jnp.concatenate(pieces, axis=0) + at_corners * scale, 0.0)
    work = jnp.where(lane == row + every, 1.0, work)
    for j in range(0, every, 2):
        top, next_row = work[j : j + 1, :], work[j + 1 : j + 2, :]
        p, q, r = spread_lane(top, j), spread_lane(top, j + 1), spread_lane(next_row, j + 1)
        inverse_p, inverse_det = 1.0 / p, 1.0 / (p * r - q * q)
        first, second = (top * r - next_row * q) * inverse_det, (next_row * p - top * q) * inverse_det
        left, right = spread_lane(work, j), spread_lane(work, j + 1)
        below = row > j + 1
        update = jnp.where(below, left, 0.0) * first + jnp.where(below, right, 0.0) * second
        work = work - update - jnp.where(row == j + 1, left, 0.0) * (top * inverse_p)
    diagonal = jnp.sum(jnp.where(lane == row, work, 0.0), axis=1, keepdims=True)
    inverse = work * (1.0 / jnp.sqrt(diagonal))
    for i in range(count):
        mine = jnp.sum(jnp.where(row == place_ref[0] * count + i, inverse, 0.0), axis=0, keepdims=True)
        upright = jnp.sum(jnp.where(lane == row + every, mine, 0.0), axis=1, keepdims=True)
        factors_ref[i] = jnp.broadcast_to(upright, (every, 128))
        basis = jnp.sum(upright * sites, axis=0, keepdims=True)
        for c in range(4):
            value = jnp.sum(jnp.where(lane[0:1] == place_ref[3] + c, basis, 0.0), axis=1, keepdims=True)
            corners_ref[4 * i + c : 4 * i + c + 1, :] = jnp.where(lane[0:1] == (127 if c % 2 else 0), value, 0.0)


def combine_kernel(factors_ref, corners_ref, place_ref, *refs):
    *tiles, out_ref = refs
    strips, count, deep, cols = tiles[0].shape
    starts = [(place_ref[0] ^ q) * count for q in range(len(tiles))]

    def one_strip(s, carry):
        rows = pl.ds(pl.multiple_of(s * deep, deep), deep)
        for c in range(0, cols, 256):
            parts = [slice(c, c + 128), slice(c + 128, c + 256)]
            totals = [[jnp.zeros((deep, 128), jnp.float32) for _ in parts] for _ in range(count)]
            for start, tile in zip(starts, tiles):
                for k in range(count):
                    fields = [tile[s, k, :, lanes] for lanes in parts]
                    for i in range(count):
                        factor = factors_ref[i, pl.ds(start + k, deep, stride=0), :]
                        totals[i] = [total + factor * field for total, field in zip(totals[i], fields)]
            for i in range(count):
                for lanes, total in zip(parts, totals[i]):
                    out_ref[i, rows, lanes] = total
        return carry

    lax.fori_loop(0, strips, one_strip, 0, unroll=True)
    last = strips * deep - 1
    for i in range(count):
        for c, (row, first) in enumerate([(0, 0), (0, cols - 128), (last, 0), (last, cols - 128)]):
            at = (slice(row, row + 1), slice(first, first + 128))
            out_ref[i, *at] = out_ref[i, *at] + corners_ref[4 * i + c : 4 * i + c + 1, :]


def swapped(value, axis, partner):
    return lax.ppermute(value, axis, [(i, partner(i)) for i in range(lax.axis_size(axis))])


def near_and_far(near, far, axis):
    size = lax.axis_size(axis)
    near = swapped(near, axis, lambda i: i ^ 1)
    return near, swapped(far, axis, lambda i: (i + (1 if i % 2 else -1)) % size)


def in_vmem(*values):
    return [pltpu.with_memory_space_constraint(v, pltpu.VMEM) for v in values]


def body(vectors, levels, level_table, filter_low, filter_high):
    count, rows, cols = vectors.shape
    groups = lax.axis_size("grp")
    every = count * groups
    deep = rows // groups
    packed_rows = 2 * (count + 1) * (cols // 128)
    here_x, here_y = lax.axis_index("lx"), lax.axis_index("ly")
    size_x, size_y = lax.axis_size("lx"), lax.axis_size("ly")
    beyond = [
        4 * ((here_x + dx) % size_x * size_y + (here_y + dy) % size_y) + 3 - c
        for c, (dx, dy) in enumerate([(-1, -1), (-1, 1), (1, -1), (1, 1)])
    ]
    place = jnp.stack([lax.axis_index("grp"), here_x % 2, here_y % 2, 4 * (here_x * size_y + here_y), *beyond])
    row_ends, col_ends = rows // 8 - 1, cols // 128 - 1
    hbm_vectors, hbm_levels = (pltpu.with_memory_space_constraint(v, pltpu.HBM) for v in (vectors, levels))
    near_rows, far_rows, near, far = pl.pallas_call(
        edges_kernel,
        grid=(1,),
        out_shape=(vmem_shape_of(packed_rows, 128),) * 2 + (vmem_shape_of(8, 128),) * 2,
        in_specs=[
            SMEM,
            pl.BlockSpec((count, 8, cols), lambda i: (0, 0, 0)),
            pl.BlockSpec((count, 8, cols), lambda i: (0, row_ends, 0)),
            pl.BlockSpec((count, rows, 128), lambda i: (0, 0, 0)),
            pl.BlockSpec((count, rows, 128), lambda i: (0, 0, col_ends)),
            pl.BlockSpec((8, cols), lambda i: (0, 0)),
            pl.BlockSpec((8, cols), lambda i: (row_ends, 0)),
            pl.BlockSpec((rows, 128), lambda i: (0, 0)),
            pl.BlockSpec((rows, 128), lambda i: (0, col_ends)),
        ],
        out_specs=(VMEM,) * 4,
        compiler_params=COMPILER,
        name="edges",
    )(place, *[hbm_vectors] * 4, *[hbm_levels] * 4)
    near_rows, far_rows = in_vmem(*near_and_far(near_rows, far_rows, "lx"))
    near, far = in_vmem(*near_and_far(near, far, "ly"))
    strips, corner = pl.pallas_call(
        filter_kernel,
        out_shape=(vmem_shape_of(groups, count, deep, cols), vmem_shape_of(8, 128)),
        in_specs=[SMEM, VMEM, VMEM, SMEM] + [VMEM] * 4 + [SMEM] * 2,
        out_specs=(VMEM, VMEM),
        compiler_params=COMPILER,
        name="filter",
    )(place, vectors, levels, level_table, near_rows, far_rows, near, far, filter_low, filter_high)
    mine = lax.all_to_all(strips, "grp", 0, 0).reshape(every, deep, cols)
    strips, mine = lax.optimization_barrier((strips, mine))
    tiles = {q: swapped(strips, "grp", lambda i, q=q: i ^ q) for q in (1, 4, 2, 6)}
    tiles[0] = strips
    planes = lax.axis_size("lx") * lax.axis_size("ly")
    total = rows * cols * planes
    gram = pl.pallas_call(
        lambda *refs: gram_kernel(1.0 / total, *refs),
        out_shape=vmem_shape_of(planes, 8 + count, 128),
        in_specs=[VMEM, VMEM],
        out_specs=VMEM,
        compiler_params=COMPILER,
        name="gram",
    )(*in_vmem(mine), corner)
    gram = jnp.sum(lax.all_to_all(gram, ("lx", "ly"), 0, 0), axis=0)
    grams = lax.all_to_all(jnp.broadcast_to(gram[None], (groups,) + gram.shape), "grp", 0, 0)
    grams, tiles = lax.optimization_barrier((grams, tiles))
    for q in range(2, groups, 2):
        tiles[q + 1] = swapped(tiles[q], "grp", lambda i: i ^ 1)
    factors, corners = pl.pallas_call(
        lambda *refs: factor_kernel(1.0 / total, *refs),
        out_shape=(vmem_shape_of(count, every, 128), vmem_shape_of(4 * count, 128)),
        in_specs=[VMEM, SMEM],
        out_specs=(VMEM, VMEM),
        compiler_params=COMPILER,
        name="factor",
    )(*in_vmem(grams), place)
    return pl.pallas_call(
        combine_kernel,
        out_shape=shape_of(count, rows, cols),
        in_specs=[VMEM, VMEM, SMEM] + [VMEM] * groups,
        out_specs=VMEM,
        compiler_params=COMPILER,
        name="combine",
    )(factors, corners, place, *in_vmem(*[tiles[q] for q in range(groups)]))


def solution(mesh):
    in_specs = (P("grp", "lx", "ly"), P("lx", "ly"), P(), P(), P())
    out_specs = P("grp", "lx", "ly")
    return jax.shard_map(body, mesh=mesh, in_specs=in_specs, out_specs=out_specs, check_vma=False)
```

```python
import jax
import jax.numpy as jnp
from jax import lax
from jax.experimental import pallas as pl
from jax.experimental.pallas import tpu as pltpu
from jax.sharding import PartitionSpec as P

HIGHEST = lax.Precision.HIGHEST
VMEM = pl.BlockSpec(memory_space=pltpu.VMEM)
SMEM = pl.BlockSpec(memory_space=pltpu.SMEM)
COMPILER = pltpu.CompilerParams(vmem_limit_bytes=16 * 1024 * 1024)


def shape_of(*dims):
    return jax.ShapeDtypeStruct(dims, jnp.float32)


def vmem_shape_of(*dims):
    return pltpu.VMEM(dims, jnp.float32)


def onsite_of(levels, table_ref):
    onsite = jnp.zeros(levels.shape, jnp.float32)
    for k in range(table_ref.shape[0]):
        onsite = jnp.where(levels == k, table_ref[k], onsite)
    return onsite


def halo_rows(near_ref, far_ref, even, j, parts, chosen):
    tiles = []
    for c in chosen:
        at = 2 * (j * parts + c)
        near, far = near_ref[at : at + 2, :], far_ref[at : at + 2, :]
        tiles.append(
            jnp.concatenate(
                [jnp.where(even, near, far), jnp.zeros((4, 128), jnp.float32), jnp.where(even, far, near)], axis=0
            )
        )
    return jnp.concatenate(tiles, axis=1)


def packed_lanes(x):
    groups = x.shape[0] // 8
    blocks = []
    for start in range(0, groups, 8):
        block = x[8 * start : 8 * start + 8]
        for t in range(1, min(8, groups - start)):
            block = block + pltpu.roll(x[8 * (start + t) : 8 * (start + t) + 8], 16 * t, 1)
        blocks.append(block)
    return jnp.concatenate(blocks, axis=1)


def unpacked_lanes(x, groups):
    tiles = []
    for t in range(groups):
        block = x[:, 128 * (t // 8) : 128 * (t // 8) + 128]
        tiles.append(pltpu.roll(block, 128 - 16 * (t % 8), 1) if t % 8 else block)
    return jnp.concatenate(tiles, axis=0)


def edges_kernel(
    place_ref, top_ref, end_ref, left_ref, right_ref, top_levels_ref, end_levels_ref, left_levels_ref, right_levels_ref,
    near_rows_ref, far_rows_ref, near_cols_ref, far_cols_ref,
):
    even_row, even_col = place_ref[1] == 0, place_ref[2] == 0
    count, deep = top_ref.shape[0], top_ref.shape[1]
    parts = top_ref.shape[2] // 128
    top_levels = top_levels_ref[...].astype(jnp.float32)
    end_levels = end_levels_ref[...].astype(jnp.float32)
    for j in range(count + 1):
        first = top_ref[j, 0:2, :] if j < count else top_levels[0:2]
        last = end_ref[j, deep - 2 : deep, :] if j < count else end_levels[deep - 2 : deep]
        near, far = jnp.where(even_row, last, first), jnp.where(even_row, first, last)
        for c in range(parts):
            at = 2 * (j * parts + c)
            near_rows_ref[at : at + 2, :] = near[:, c * 128 : c * 128 + 128]
            far_rows_ref[at : at + 2, :] = far[:, c * 128 : c * 128 + 128]
    rows = left_ref.shape[1]
    lane = lax.broadcasted_iota(jnp.int32, (rows, 128), 1)
    first = jnp.zeros((rows, 128), jnp.float32)
    last = jnp.zeros((rows, 128), jnp.float32)
    for j in range(count + 1):
        left = left_ref[j] if j < count else left_levels_ref[...].astype(jnp.float32)
        right = right_ref[j] if j < count else right_levels_ref[...].astype(jnp.float32)
        if j:
            left = pltpu.roll(left, 2 * j, 1)
            right = pltpu.roll(right, 128 - 2 * j, 1)
        first = jnp.where(lane // 2 == j, left, first)
        last = jnp.where((127 - lane) // 2 == j, right, last)
    first, last = packed_lanes(first), packed_lanes(last)
    near_cols_ref[...] = jnp.where(even_col, last, first)
    far_cols_ref[...] = jnp.where(even_col, first, last)


def filter_kernel(
    place_ref, v_ref, levels_ref, table_ref, near_rows_ref, far_rows_ref, near_ref, far_ref, low_ref, high_ref, out_ref, corner_ref
):
    even_row, even_col = place_ref[1] == 0, place_ref[2] == 0
    count, rows, cols = v_ref.shape
    strips = out_ref.shape[0]
    deep = rows // strips
    lane = lax.broadcasted_iota(jnp.int32, (rows, 128), 1)
    parts = cols // 128
    near, far = near_ref[...], far_ref[...]
    after = unpacked_lanes(jnp.where(even_col, near, far), rows // 8)
    before = unpacked_lanes(jnp.where(even_col, far, near), rows // 8)

    def extended(own, j):
        tall = jnp.concatenate([own, halo_rows(near_rows_ref, far_rows_ref, even_row, j, parts, range(parts))], axis=0)
        right = pltpu.roll(after, 128 - 2 * j, 1) if j else after
        left = pltpu.roll(before, 2 * j, 1) if j else before
        side = jnp.concatenate([jnp.where(lane < 64, right, left), jnp.zeros((8, 128), jnp.float32)], axis=0)
        return jnp.concatenate([tall, side], axis=1)

    center = (high_ref[0] + low_ref[0]) / 2.0
    half = jnp.full((1, 1), (high_ref[0] - low_ref[0]) * 0.5, jnp.float32)
    scale = 1.0 / half
    weight = (onsite_of(extended(levels_ref[...].astype(jnp.float32), count), table_ref) - center) * scale

    def scaled_operator(x):
        height, width = x.shape
        beside = (pltpu.roll(x, 1, 0) + pltpu.roll(x, height - 1, 0)) + (
            pltpu.roll(x, 1, 1) + pltpu.roll(x, width - 1, 1)
        )
        return weight * x - scale * beside

    site = lax.broadcasted_iota(jnp.int32, (1, 128), 1)
    row_at = lax.broadcasted_iota(jnp.int32, (rows, cols), 0)
    col_at = lax.broadcasted_iota(jnp.int32, (rows, cols), 1)
    inside = ((row_at > 0) & (row_at < rows - 1)) | ((col_at > 0) & (col_at < cols - 1))
    corners = [(0, 0), (0, cols - 1), (rows - 1, 0), (rows - 1, cols - 1)]
    corner_ref[...] = jnp.zeros(corner_ref.shape, jnp.float32)
    for j in range(count):
        own = v_ref[j]
        x = extended(own, j)
        filtered = (2.0 * scaled_operator(scaled_operator(x)) - x)[:rows, :cols]
        held = jnp.zeros((1, 128), jnp.float32)
        for c, (r, l) in enumerate(corners):
            held = held + jnp.where(site == place_ref[3] + c, filtered[r : r + 1, l : l + 1], 0.0)
            held = held + jnp.where(site == place_ref[4 + c], 4.0 * scale * scale * own[r : r + 1, l : l + 1], 0.0)
        corner_ref[j : j + 1, :] = held
        filtered = jnp.where(inside, filtered, 0.0)
        for s in range(strips):
            out_ref[s, j] = filtered[s * deep : (s + 1) * deep]


def gram_kernel(scale, x_ref, corner_ref, out_ref):
    count, deep, cols = x_ref.shape
    gram = jnp.zeros((count, 128), jnp.float32)
    none = jnp.zeros((128 - count, cols), jnp.float32)
    for r in range(deep):
        x = x_ref[:, r, :]
        gram = gram + lax.dot_general(
            x, jnp.concatenate([x, none], axis=0), (((1,), (1,)), ((), ())),
            precision=HIGHEST, preferred_element_type=jnp.float32,
        )
    packed = gram[0:8]
    for q in range(1, count // 8):
        packed = packed + pltpu.roll(gram[8 * q : 8 * q + 8], q * count, 1)
    both = jnp.concatenate([packed * scale, corner_ref[0 : out_ref.shape[1] - 8, :]], axis=0)
    out_ref[...] = jnp.broadcast_to(both[None], out_ref.shape)


def spread_lane(x, j):
    return jnp.broadcast_to(x[:, j : j + 1], x.shape)


def factor_kernel(scale, gram_ref, place_ref, factors_ref, corners_ref):
    count, every, _ = factors_ref.shape
    packed = gram_ref[0, 0:8, :]
    for k in range(1, gram_ref.shape[0]):
        packed = packed + gram_ref[k, 0:8, :]
    sites = jnp.concatenate([gram_ref[k, 8 : 8 + count, :] for k in range(gram_ref.shape[0])], axis=0)
    none = jnp.zeros((128 - every, 128), jnp.float32)
    at_corners = lax.dot_general(
        sites, jnp.concatenate([sites, none], axis=0), (((1,), (1,)), ((), ())),
        precision=HIGHEST, preferred_element_type=jnp.float32,
    )
    pieces = [packed] + [pltpu.roll(packed, 128 - q * every, 1) for q in range(1, every // 8)]
    row = lax.broadcasted_iota(jnp.int32, (every, 128), 0)
    lane = lax.broadcasted_iota(jnp.int32, (every, 128), 1)
    work = jnp.where(lane < every, jnp.concatenate(pieces, axis=0) + at_corners * scale, 0.0)
    work = jnp.where(lane == row + every, 1.0, work)
    for j in range(0, every, 2):
        top, next_row = work[j : j + 1, :], work[j + 1 : j + 2, :]
        p, q, r = spread_lane(top, j), spread_lane(top, j + 1), spread_lane(next_row, j + 1)
        inverse_p, inverse_det = 1.0 / p, 1.0 / (p * r - q * q)
        first, second = (top * r - next_row * q) * inverse_det, (next_row * p - top * q) * inverse_det
        left, right = spread_lane(work, j), spread_lane(work, j + 1)
        below = row > j + 1
        update = jnp.where(below, left, 0.0) * first + jnp.where(below, right, 0.0) * second
        work = work - update - jnp.where(row == j + 1, left, 0.0) * (top * inverse_p)
    diagonal = jnp.sum(jnp.where(lane == row, work, 0.0), axis=1, keepdims=True)
    inverse = work * (1.0 / jnp.sqrt(diagonal))
    for i in range(count):
        mine = jnp.sum(jnp.where(row == place_ref[0] * count + i, inverse, 0.0), axis=0, keepdims=True)
        upright = jnp.sum(jnp.where(lane == row + every, mine, 0.0), axis=1, keepdims=True)
        factors_ref[i] = jnp.broadcast_to(upright, (every, 128))
        basis = jnp.sum(upright * sites, axis=0, keepdims=True)
        for c in range(4):
            value = jnp.sum(jnp.where(lane[0:1] == place_ref[3] + c, basis, 0.0), axis=1, keepdims=True)
            corners_ref[4 * i + c : 4 * i + c + 1, :] = jnp.where(lane[0:1] == (127 if c % 2 else 0), value, 0.0)


def combine_kernel(factors_ref, corners_ref, place_ref, *refs):
    *tiles, out_ref = refs
    strips, count, deep, cols = tiles[0].shape
    starts = [(place_ref[0] ^ q) * count for q in range(len(tiles))]

    def one_strip(s, carry):
        rows = pl.ds(pl.multiple_of(s * deep, deep), deep)
        for c in range(0, cols, 256):
            parts = [slice(c, c + 128), slice(c + 128, c + 256)]
            totals = [[jnp.zeros((deep, 128), jnp.float32) for _ in parts] for _ in range(count)]
            for start, tile in zip(starts, tiles):
                for k in range(count):
                    fields = [tile[s, k, :, lanes] for lanes in parts]
                    for i in range(count):
                        factor = jnp.broadcast_to(factors_ref[i, pl.ds(start + k, 1), :], (deep, 128))
                        totals[i] = [total + factor * field for total, field in zip(totals[i], fields)]
            for i in range(count):
                for lanes, total in zip(parts, totals[i]):
                    out_ref[i, rows, lanes] = total
        return carry

    lax.fori_loop(0, strips, one_strip, 0, unroll=True)
    last = strips * deep - 1
    for i in range(count):
        for c, (row, first) in enumerate([(0, 0), (0, cols - 128), (last, 0), (last, cols - 128)]):
            at = (slice(row, row + 1), slice(first, first + 128))
            out_ref[i, *at] = out_ref[i, *at] + corners_ref[4 * i + c : 4 * i + c + 1, :]


def swapped(value, axis, partner):
    return lax.ppermute(value, axis, [(i, partner(i)) for i in range(lax.axis_size(axis))])


def near_and_far(near, far, axis):
    size = lax.axis_size(axis)
    near = swapped(near, axis, lambda i: i ^ 1)
    return near, swapped(far, axis, lambda i: (i + (1 if i % 2 else -1)) % size)


def in_vmem(*values):
    return [pltpu.with_memory_space_constraint(v, pltpu.VMEM) for v in values]


def body(vectors, levels, level_table, filter_low, filter_high):
    count, rows, cols = vectors.shape
    groups = lax.axis_size("grp")
    every = count * groups
    deep = rows // groups
    packed_rows = 2 * (count + 1) * (cols // 128)
    here_x, here_y = lax.axis_index("lx"), lax.axis_index("ly")
    size_x, size_y = lax.axis_size("lx"), lax.axis_size("ly")
    beyond = [
        4 * ((here_x + dx) % size_x * size_y + (here_y + dy) % size_y) + 3 - c
        for c, (dx, dy) in enumerate([(-1, -1), (-1, 1), (1, -1), (1, 1)])
    ]
    place = jnp.stack([lax.axis_index("grp"), here_x % 2, here_y % 2, 4 * (here_x * size_y + here_y), *beyond])
    row_ends, col_ends = rows // 8 - 1, cols // 128 - 1
    hbm_vectors, hbm_levels = (pltpu.with_memory_space_constraint(v, pltpu.HBM) for v in (vectors, levels))
    near_rows, far_rows, near, far = pl.pallas_call(
        edges_kernel,
        grid=(1,),
        out_shape=(vmem_shape_of(packed_rows, 128),) * 2 + (vmem_shape_of(8, 128),) * 2,
        in_specs=[
            SMEM,
            pl.BlockSpec((count, 8, cols), lambda i: (0, 0, 0)),
            pl.BlockSpec((count, 8, cols), lambda i: (0, row_ends, 0)),
            pl.BlockSpec((count, rows, 128), lambda i: (0, 0, 0)),
            pl.BlockSpec((count, rows, 128), lambda i: (0, 0, col_ends)),
            pl.BlockSpec((8, cols), lambda i: (0, 0)),
            pl.BlockSpec((8, cols), lambda i: (row_ends, 0)),
            pl.BlockSpec((rows, 128), lambda i: (0, 0)),
            pl.BlockSpec((rows, 128), lambda i: (0, col_ends)),
        ],
        out_specs=(VMEM,) * 4,
        compiler_params=COMPILER,
        name="edges",
    )(place, *[hbm_vectors] * 4, *[hbm_levels] * 4)
    near_rows, far_rows = in_vmem(*near_and_far(near_rows, far_rows, "lx"))
    near, far = in_vmem(*near_and_far(near, far, "ly"))
    strips, corner = pl.pallas_call(
        filter_kernel,
        out_shape=(vmem_shape_of(groups, count, deep, cols), vmem_shape_of(8, 128)),
        in_specs=[SMEM, VMEM, VMEM, SMEM] + [VMEM] * 4 + [SMEM] * 2,
        out_specs=(VMEM, VMEM),
        compiler_params=COMPILER,
        name="filter",
    )(place, vectors, levels, level_table, near_rows, far_rows, near, far, filter_low, filter_high)
    mine = lax.all_to_all(strips, "grp", 0, 0).reshape(every, deep, cols)
    strips, mine = lax.optimization_barrier((strips, mine))
    tiles = {q: swapped(strips, "grp", lambda i, q=q: i ^ q) for q in (1, 4, 2, 6)}
    tiles[0] = strips
    planes = lax.axis_size("lx") * lax.axis_size("ly")
    total = rows * cols * planes
    gram = pl.pallas_call(
        lambda *refs: gram_kernel(1.0 / total, *refs),
        out_shape=vmem_shape_of(planes, 8 + count, 128),
        in_specs=[VMEM, VMEM],
        out_specs=VMEM,
        compiler_params=COMPILER,
        name="gram",
    )(*in_vmem(mine), corner)
    gram = jnp.sum(lax.all_to_all(gram, ("lx", "ly"), 0, 0), axis=0)
    grams = lax.all_to_all(jnp.broadcast_to(gram[None], (groups,) + gram.shape), "grp", 0, 0)
    grams, tiles = lax.optimization_barrier((grams, tiles))
    for q in range(2, groups, 2):
        tiles[q + 1] = swapped(tiles[q], "grp", lambda i: i ^ 1)
    factors, corners = pl.pallas_call(
        lambda *refs: factor_kernel(1.0 / total, *refs),
        out_shape=(vmem_shape_of(count, every, 128), vmem_shape_of(4 * count, 128)),
        in_specs=[VMEM, SMEM],
        out_specs=(VMEM, VMEM),
        compiler_params=COMPILER,
        name="factor",
    )(*in_vmem(grams), place)
    return pl.pallas_call(
        combine_kernel,
        out_shape=shape_of(count, rows, cols),
        in_specs=[VMEM, VMEM, SMEM] + [VMEM] * groups,
        out_specs=VMEM,
        compiler_params=COMPILER,
        name="combine",
    )(factors, corners, place, *in_vmem(*[tiles[q] for q in range(groups)]))


def solution(mesh):
    in_specs = (P("grp", "lx", "ly"), P("lx", "ly"), P(), P(), P())
    out_specs = P("grp", "lx", "ly")
    return jax.shard_map(body, mesh=mesh, in_specs=in_specs, out_specs=out_specs, check_vma=False)
```

```python
import jax
import jax.numpy as jnp
from jax import lax
from jax.experimental import pallas as pl
from jax.experimental.pallas import tpu as pltpu
from jax.sharding import PartitionSpec as P

HIGHEST = lax.Precision.HIGHEST
VMEM = pl.BlockSpec(memory_space=pltpu.VMEM)
SMEM = pl.BlockSpec(memory_space=pltpu.SMEM)
COMPILER = pltpu.CompilerParams(vmem_limit_bytes=16 * 1024 * 1024)


def shape_of(*dims):
    return jax.ShapeDtypeStruct(dims, jnp.float32)


def vmem_shape_of(*dims):
    return pltpu.VMEM(dims, jnp.float32)


def onsite_of(levels, table_ref):
    onsite = jnp.zeros(levels.shape, jnp.float32)
    for k in range(table_ref.shape[0]):
        onsite = jnp.where(levels == k, table_ref[k], onsite)
    return onsite


def halo_rows(near_ref, far_ref, even, j, parts, chosen):
    tiles = []
    for c in chosen:
        at = 2 * (j * parts + c)
        near, far = near_ref[at : at + 2, :], far_ref[at : at + 2, :]
        tiles.append(
            jnp.concatenate(
                [jnp.where(even, near, far), jnp.zeros((4, 128), jnp.float32), jnp.where(even, far, near)], axis=0
            )
        )
    return jnp.concatenate(tiles, axis=1)


def packed_lanes(x):
    groups = x.shape[0] // 8
    blocks = []
    for start in range(0, groups, 8):
        block = x[8 * start : 8 * start + 8]
        for t in range(1, min(8, groups - start)):
            block = block + pltpu.roll(x[8 * (start + t) : 8 * (start + t) + 8], 16 * t, 1)
        blocks.append(block)
    return jnp.concatenate(blocks, axis=1)


def unpacked_lanes(x, groups):
    tiles = []
    for t in range(groups):
        block = x[:, 128 * (t // 8) : 128 * (t // 8) + 128]
        tiles.append(pltpu.roll(block, 128 - 16 * (t % 8), 1) if t % 8 else block)
    return jnp.concatenate(tiles, axis=0)


def edges_kernel(
    place_ref, top_ref, end_ref, left_ref, right_ref, top_levels_ref, end_levels_ref, left_levels_ref, right_levels_ref,
    near_rows_ref, far_rows_ref, near_cols_ref, far_cols_ref,
):
    even_row, even_col = place_ref[1] == 0, place_ref[2] == 0
    count, deep = top_ref.shape[0], top_ref.shape[1]
    parts = top_ref.shape[2] // 128
    top_levels = top_levels_ref[...].astype(jnp.float32)
    end_levels = end_levels_ref[...].astype(jnp.float32)
    for j in range(count + 1):
        first = top_ref[j, 0:2, :] if j < count else top_levels[0:2]
        last = end_ref[j, deep - 2 : deep, :] if j < count else end_levels[deep - 2 : deep]
        near, far = jnp.where(even_row, last, first), jnp.where(even_row, first, last)
        for c in range(parts):
            at = 2 * (j * parts + c)
            near_rows_ref[at : at + 2, :] = near[:, c * 128 : c * 128 + 128]
            far_rows_ref[at : at + 2, :] = far[:, c * 128 : c * 128 + 128]
    rows = left_ref.shape[1]
    lane = lax.broadcasted_iota(jnp.int32, (rows, 128), 1)
    first = jnp.zeros((rows, 128), jnp.float32)
    last = jnp.zeros((rows, 128), jnp.float32)
    for j in range(count + 1):
        left = left_ref[j] if j < count else left_levels_ref[...].astype(jnp.float32)
        right = right_ref[j] if j < count else right_levels_ref[...].astype(jnp.float32)
        if j:
            left = pltpu.roll(left, 2 * j, 1)
            right = pltpu.roll(right, 128 - 2 * j, 1)
        first = jnp.where(lane // 2 == j, left, first)
        last = jnp.where((127 - lane) // 2 == j, right, last)
    first, last = packed_lanes(first), packed_lanes(last)
    near_cols_ref[...] = jnp.where(even_col, last, first)
    far_cols_ref[...] = jnp.where(even_col, first, last)


def filter_kernel(
    place_ref, v_ref, levels_ref, table_ref, near_rows_ref, far_rows_ref, near_ref, far_ref, low_ref, high_ref, out_ref, corner_ref
):
    even_row, even_col = place_ref[1] == 0, place_ref[2] == 0
    count, rows, cols = v_ref.shape
    strips = out_ref.shape[0]
    deep = rows // strips
    lane = lax.broadcasted_iota(jnp.int32, (rows, 128), 1)
    parts = cols // 128
    near, far = near_ref[...], far_ref[...]
    after = unpacked_lanes(jnp.where(even_col, near, far), rows // 8)
    before = unpacked_lanes(jnp.where(even_col, far, near), rows // 8)

    def extended(own, j):
        tall = jnp.concatenate([own, halo_rows(near_rows_ref, far_rows_ref, even_row, j, parts, range(parts))], axis=0)
        right = pltpu.roll(after, 128 - 2 * j, 1) if j else after
        left = pltpu.roll(before, 2 * j, 1) if j else before
        side = jnp.concatenate([jnp.where(lane < 64, right, left), jnp.zeros((8, 128), jnp.float32)], axis=0)
        return jnp.concatenate([tall, side], axis=1)

    center = (high_ref[0] + low_ref[0]) / 2.0
    half = jnp.full((1, 1), (high_ref[0] - low_ref[0]) * 0.5, jnp.float32)
    scale = 1.0 / half
    weight = (onsite_of(extended(levels_ref[...].astype(jnp.float32), count), table_ref) - center) * scale

    def scaled_operator(x):
        height, width = x.shape
        beside = (pltpu.roll(x, 1, 0) + pltpu.roll(x, height - 1, 0)) + (
            pltpu.roll(x, 1, 1) + pltpu.roll(x, width - 1, 1)
        )
        return weight * x - scale * beside

    site = lax.broadcasted_iota(jnp.int32, (1, 128), 1)
    row_at = lax.broadcasted_iota(jnp.int32, (rows, cols), 0)
    col_at = lax.broadcasted_iota(jnp.int32, (rows, cols), 1)
    inside = ((row_at > 0) & (row_at < rows - 1)) | ((col_at > 0) & (col_at < cols - 1))
    corners = [(0, 0), (0, cols - 1), (rows - 1, 0), (rows - 1, cols - 1)]
    corner_ref[...] = jnp.zeros(corner_ref.shape, jnp.float32)
    for j in range(count):
        own = v_ref[j]
        x = extended(own, j)
        filtered = (2.0 * scaled_operator(scaled_operator(x)) - x)[:rows, :cols]
        held = jnp.zeros((1, 128), jnp.float32)
        for c, (r, l) in enumerate(corners):
            held = held + jnp.where(site == place_ref[3] + c, filtered[r : r + 1, l : l + 1], 0.0)
            held = held + jnp.where(site == place_ref[4 + c], 4.0 * scale * scale * own[r : r + 1, l : l + 1], 0.0)
        corner_ref[j : j + 1, :] = held
        filtered = jnp.where(inside, filtered, 0.0)
        for s in range(strips):
            out_ref[s, j] = filtered[s * deep : (s + 1) * deep]


def gram_kernel(scale, x_ref, corner_ref, out_ref):
    count, deep, cols = x_ref.shape
    gram = jnp.zeros((count, 128), jnp.float32)
    none = jnp.zeros((128 - count, cols), jnp.float32)
    for r in range(deep):
        x = x_ref[:, r, :]
        gram = gram + lax.dot_general(
            x, jnp.concatenate([x, none], axis=0), (((1,), (1,)), ((), ())),
            precision=HIGHEST, preferred_element_type=jnp.float32,
        )
    packed = gram[0:8]
    for q in range(1, count // 8):
        packed = packed + pltpu.roll(gram[8 * q : 8 * q + 8], q * count, 1)
    both = jnp.concatenate([packed * scale, corner_ref[0 : out_ref.shape[1] - 8, :]], axis=0)
    out_ref[...] = jnp.broadcast_to(both[None], out_ref.shape)


def spread_lane(x, j):
    return jnp.broadcast_to(x[:, j : j + 1], x.shape)


def factor_kernel(scale, gram_ref, place_ref, factors_ref, corners_ref):
    count, every, _ = factors_ref.shape
    packed = gram_ref[0, 0:8, :]
    for k in range(1, gram_ref.shape[0]):
        packed = packed + gram_ref[k, 0:8, :]
    sites = jnp.concatenate([gram_ref[k, 8 : 8 + count, :] for k in range(gram_ref.shape[0])], axis=0)
    none = jnp.zeros((128 - every, 128), jnp.float32)
    at_corners = lax.dot_general(
        sites, jnp.concatenate([sites, none], axis=0), (((1,), (1,)), ((), ())),
        precision=HIGHEST, preferred_element_type=jnp.float32,
    )
    pieces = [packed] + [pltpu.roll(packed, 128 - q * every, 1) for q in range(1, every // 8)]
    row = lax.broadcasted_iota(jnp.int32, (every, 128), 0)
    lane = lax.broadcasted_iota(jnp.int32, (every, 128), 1)
    work = jnp.where(lane < every, jnp.concatenate(pieces, axis=0) + at_corners * scale, 0.0)
    work = jnp.where(lane == row + every, 1.0, work)
    for j in range(0, every, 2):
        top, next_row = work[j : j + 1, :], work[j + 1 : j + 2, :]
        p, q, r = spread_lane(top, j), spread_lane(top, j + 1), spread_lane(next_row, j + 1)
        inverse_p, inverse_det = 1.0 / p, 1.0 / (p * r - q * q)
        first, second = (top * r - next_row * q) * inverse_det, (next_row * p - top * q) * inverse_det
        left, right = spread_lane(work, j), spread_lane(work, j + 1)
        below = row > j + 1
        update = jnp.where(below, left, 0.0) * first + jnp.where(below, right, 0.0) * second
        work = work - update - jnp.where(row == j + 1, left, 0.0) * (top * inverse_p)
    diagonal = jnp.sum(jnp.where(lane == row, work, 0.0), axis=1, keepdims=True)
    inverse = work * (1.0 / jnp.sqrt(diagonal))
    for i in range(count):
        mine = jnp.sum(jnp.where(row == place_ref[0] * count + i, inverse, 0.0), axis=0, keepdims=True)
        upright = jnp.sum(jnp.where(lane == row + every, mine, 0.0), axis=1, keepdims=True)
        factors_ref[i] = jnp.broadcast_to(upright, (every, 128))
        basis = jnp.sum(upright * sites, axis=0, keepdims=True)
        for c in range(4):
            value = jnp.sum(jnp.where(lane[0:1] == place_ref[3] + c, basis, 0.0), axis=1, keepdims=True)
            corners_ref[4 * i + c : 4 * i + c + 1, :] = jnp.where(lane[0:1] == (127 if c % 2 else 0), value, 0.0)


def combine_kernel(factors_ref, corners_ref, place_ref, *refs):
    *tiles, out_ref = refs
    strips, count, deep, cols = tiles[0].shape
    starts = [(place_ref[0] ^ q) * count for q in range(len(tiles))]

    def one_strip(s, carry):
        rows = pl.ds(pl.multiple_of(s * deep, deep), deep)
        for c in range(0, cols, 256):
            parts = [slice(c, c + 128), slice(c + 128, c + 256)]
            totals = [[jnp.zeros((deep, 128), jnp.float32) for _ in parts] for _ in range(count)]
            for start, tile in zip(starts, tiles):
                for k in range(count):
                    fields = [tile[s, k, :, lanes] for lanes in parts]
                    for i in range(count):
                        factor = jnp.broadcast_to(factors_ref[i, pl.ds(start + k, 1), :], (deep, 128))
                        totals[i] = [total + factor * field for total, field in zip(totals[i], fields)]
            for i in range(count):
                for lanes, total in zip(parts, totals[i]):
                    out_ref[i, rows, lanes] = total
        return carry

    lax.fori_loop(0, strips, one_strip, 0, unroll=True)
    last = strips * deep - 1
    for i in range(count):
        for c, (row, first) in enumerate([(0, 0), (0, cols - 128), (last, 0), (last, cols - 128)]):
            at = (slice(row, row + 1), slice(first, first + 128))
            out_ref[i, *at] = out_ref[i, *at] + corners_ref[4 * i + c : 4 * i + c + 1, :]


def swapped(value, axis, partner):
    return lax.ppermute(value, axis, [(i, partner(i)) for i in range(lax.axis_size(axis))])


def near_and_far(near, far, axis):
    size = lax.axis_size(axis)
    near = swapped(near, axis, lambda i: i ^ 1)
    return near, swapped(far, axis, lambda i: (i + (1 if i % 2 else -1)) % size)


def in_vmem(*values):
    return [pltpu.with_memory_space_constraint(v, pltpu.VMEM) for v in values]


def body(vectors, levels, level_table, filter_low, filter_high):
    count, rows, cols = vectors.shape
    groups = lax.axis_size("grp")
    every = count * groups
    deep = rows // groups
    packed_rows = 2 * (count + 1) * (cols // 128)
    here_x, here_y = lax.axis_index("lx"), lax.axis_index("ly")
    size_x, size_y = lax.axis_size("lx"), lax.axis_size("ly")
    beyond = [
        4 * ((here_x + dx) % size_x * size_y + (here_y + dy) % size_y) + 3 - c
        for c, (dx, dy) in enumerate([(-1, -1), (-1, 1), (1, -1), (1, 1)])
    ]
    place = jnp.stack([lax.axis_index("grp"), here_x % 2, here_y % 2, 4 * (here_x * size_y + here_y), *beyond])
    row_ends, col_ends = rows // 8 - 1, cols // 128 - 1
    hbm_vectors, hbm_levels = (pltpu.with_memory_space_constraint(v, pltpu.HBM) for v in (vectors, levels))
    near_rows, far_rows, near, far = pl.pallas_call(
        edges_kernel,
        grid=(1,),
        out_shape=(vmem_shape_of(packed_rows, 128),) * 2 + (vmem_shape_of(8, 128),) * 2,
        in_specs=[
            SMEM,
            pl.BlockSpec((count, 8, cols), lambda i: (0, 0, 0)),
            pl.BlockSpec((count, 8, cols), lambda i: (0, row_ends, 0)),
            pl.BlockSpec((count, rows, 128), lambda i: (0, 0, 0)),
            pl.BlockSpec((count, rows, 128), lambda i: (0, 0, col_ends)),
            pl.BlockSpec((8, cols), lambda i: (0, 0)),
            pl.BlockSpec((8, cols), lambda i: (row_ends, 0)),
            pl.BlockSpec((rows, 128), lambda i: (0, 0)),
            pl.BlockSpec((rows, 128), lambda i: (0, col_ends)),
        ],
        out_specs=(VMEM,) * 4,
        compiler_params=COMPILER,
        name="edges",
    )(place, *[hbm_vectors] * 4, *[hbm_levels] * 4)
    near_rows, far_rows = in_vmem(*near_and_far(near_rows, far_rows, "lx"))
    near, far = in_vmem(*near_and_far(near, far, "ly"))
    strips, corner = pl.pallas_call(
        filter_kernel,
        out_shape=(vmem_shape_of(groups, count, deep, cols), vmem_shape_of(8, 128)),
        in_specs=[SMEM, VMEM, VMEM, SMEM] + [VMEM] * 4 + [SMEM] * 2,
        out_specs=(VMEM, VMEM),
        compiler_params=COMPILER,
        name="filter",
    )(place, vectors, levels, level_table, near_rows, far_rows, near, far, filter_low, filter_high)
    mine = lax.all_to_all(strips, "grp", 0, 0).reshape(every, deep, cols)
    strips, mine = lax.optimization_barrier((strips, mine))
    tiles = {q: swapped(strips, "grp", lambda i, q=q: i ^ q) for q in (4, 2, 6)}
    tiles[0] = strips
    planes = lax.axis_size("lx") * lax.axis_size("ly")
    total = rows * cols * planes
    gram = pl.pallas_call(
        lambda *refs: gram_kernel(1.0 / total, *refs),
        out_shape=vmem_shape_of(planes, 8 + count, 128),
        in_specs=[VMEM, VMEM],
        out_specs=VMEM,
        compiler_params=COMPILER,
        name="gram",
    )(*in_vmem(mine), corner)
    gram = jnp.sum(lax.all_to_all(gram, ("lx", "ly"), 0, 0), axis=0)
    grams = lax.all_to_all(jnp.broadcast_to(gram[None], (groups,) + gram.shape), "grp", 0, 0)
    grams, tiles = lax.optimization_barrier((grams, tiles))
    for q in range(0, groups, 2):
        tiles[q + 1] = swapped(tiles[q], "grp", lambda i: i ^ 1)
    factors, corners = pl.pallas_call(
        lambda *refs: factor_kernel(1.0 / total, *refs),
        out_shape=(vmem_shape_of(count, every, 128), vmem_shape_of(4 * count, 128)),
        in_specs=[VMEM, SMEM],
        out_specs=(VMEM, VMEM),
        compiler_params=COMPILER,
        name="factor",
    )(*in_vmem(grams), place)
    return pl.pallas_call(
        combine_kernel,
        out_shape=shape_of(count, rows, cols),
        in_specs=[VMEM, VMEM, SMEM] + [VMEM] * groups,
        out_specs=VMEM,
        compiler_params=COMPILER,
        name="combine",
    )(factors, corners, place, *in_vmem(*[tiles[q] for q in range(groups)]))


def solution(mesh):
    in_specs = (P("grp", "lx", "ly"), P("lx", "ly"), P(), P(), P())
    out_specs = P("grp", "lx", "ly")
    return jax.shard_map(body, mesh=mesh, in_specs=in_specs, out_specs=out_specs, check_vma=False)
```
